32 devices in a mesh: dp: 8 (over y, x, core), expert: 4 (over z).
Axes of the slice: x: 2, y: 2, z: 4, core: 2. Of those that a mesh axis runs over, the one named last changes fastest.
Arguments:
- cotangent: bfloat16 [32768, 2048], P(('dp', 'expert')), may hold values from -6 to 6
- route_ids: int32 [32768, 6], P(('dp', 'expert')), may hold values from 0 to 63, all different within a row; in each aligned block of 1024 rows (0 to 1023, 1024 to 2047, ...) at most 192 rows name the same one
- route_weights: float32 [32768, 6], P(('dp', 'expert')), may hold values from 0.02 to 1
- hidden: bfloat16 [8, 6144, 1408], P('expert', 'dp'), may hold values from -6 to 6
- master: float32 [1408, 8, 2048], P('dp', 'expert'), may hold values from -0.3 to 0.3
- first_moment: float32 [1408, 8, 2048], P('dp', 'expert'), may hold values from -1.2 to 1.2
- second_moment: float32 [1408, 8, 2048], P('dp', 'expert'), may hold values from 0.002 to 0.05
Outputs:
- new_master: float32 [1408, 8, 2048], P('dp', 'expert')
- new_first: float32 [1408, 8, 2048], P('dp', 'expert')
- new_second: float32 [1408, 8, 2048], P('dp', 'expert')
The draws below stay inside these ranges and needn't reach their ends.
Inputs may be any that keep to these rules, and one draw needn't show every extreme that they name: `route_ids`: each row names 6 different experts. Within the 1024 rows of one device no expert is named by more than 192 rows.
All inputs are finite; a program needn't handle non-finite values.
Results may differ from the reference program's by a relative error of at most 0.0019.
Values may be sent and summed in bfloat16 or wider, within the bound.
A program may use at most 128 MiB of HBM per device.

```python
import math
import jax
import jax.numpy as jnp
import numpy as np
from jax import lax

D = 2048
F = 1408
N_ROUTED = 64
TOP = 6
EXP_DEV = 2
TOK_DEV = 1024
CAP = 192
WINDOW = 8
TOKENS = 32768
N_DP = 8
N_EXPERT = 4


def block_scale(own_key, dims, shards, smallest, high):
    def one(dim, blocks):
        draws = jax.random.uniform(jax.random.fold_in(jax.random.fold_in(own_key, 6), dim), (blocks,), jnp.float32, smallest / len(shards), high / len(shards))
        return jnp.repeat(jnp.exp(draws), dims[dim] // blocks).reshape((-1,) + (1,) * (len(dims) - dim - 1))

    factor_of = one(*shards[0])
    for cut in shards[1:]:
        factor_of = factor_of * one(*cut)
    return factor_of


def shared_out(stream_key, own, number, rows, number_of, top, limit, lean):
    sequence = jax.random.permutation(stream_key, number_of)
    packed, usual = load_shares(number_of, rows * top, limit, lean, True), load_shares(number_of, rows * top, limit, lean, False)
    places = jnp.arange(number_of)

    def named(sizes, turn):
        used = int((sizes > 0).sum())
        fixed = max(1, used // 4)
        passed = fixed + (places - fixed + turn * (used - fixed)) % max(1, number_of - fixed)
        return jnp.zeros((number_of,), jnp.int32).at[sequence[jnp.where(places < fixed, places, passed)]].set(jnp.asarray(sizes, jnp.int32))

    sizes = jnp.where(number % 4 == 0, named(packed, number // 4), named(usual, number - number // 4 - 1))
    mixed = jax.random.permutation(jax.random.fold_in(own, 3), number_of)
    donor, sink = mixed[0:number_of // 2 * 2:2], mixed[1:number_of // 2 * 2:2]
    margin = jnp.minimum(sizes[donor] - 1, limit - sizes[sink]) // 2
    margin = jnp.where((donor == sequence[0]) | (sink == sequence[0]) | (sizes[sink] == 0), 0, jnp.maximum(margin, 0))
    passed = jax.random.randint(jax.random.fold_in(own, 4), (number_of // 2,), 0, 1 << 20) % (margin + 1)
    sizes = sizes.at[donor].add(-passed).at[sink].add(passed)
    items = jnp.searchsorted(jnp.cumsum(sizes), jnp.arange(rows * top), side="right").astype(jnp.int32)
    table = items.reshape(top, rows).T
    table = table[jax.random.permutation(jax.random.fold_in(own, 1), rows)]
    turn = jax.random.randint(jax.random.fold_in(own, 2), (rows, 1), 0, top)
    return jnp.take_along_axis(table, (jnp.arange(top)[None, :] + turn) % top, axis=1)


def load_shares(number_of, total, limit, skew, full):
    portions = [(1 << 20) // math.isqrt(standing ** skew) + 1 for standing in range(1, number_of + 1)]
    largest = limit if full else min(limit, max(-(-total // number_of), total * portions[0] // sum(portions)))
    least = 1 if total - largest >= number_of - 1 else 0
    holding, spare = [largest] + [least] * (number_of - 1), total - largest - least * (number_of - 1)
    while spare > 0:
        candidates = [i for i in range(1, number_of) if holding[i] < largest] or [i for i in range(1, number_of) if holding[i] < limit]
        pool, remaining = sum([portions[i] for i in candidates]), spare
        for i in candidates:
            addition = min(limit - holding[i], max(1, remaining * portions[i] // pool), spare)
            holding[i] = holding[i] + addition
            spare = spare - addition
    return np.array(holding)


def bell_draw(rng, shape, width, reach, pieces=(), kind=jnp.bfloat16):
    entries = width * jax.random.normal(rng, shape, jnp.float32)
    if pieces:
        entries = entries * block_scale(rng, shape, pieces, -0.22, 0.18)
    return jnp.clip(entries, -reach, reach).astype(kind)


def setup_inputs(seed: int = 0) -> dict:
    splits = jax.random.split(jax.random.key(seed), 8)
    cotangent = bell_draw(splits[0], (TOKENS, D), 1.0, 6.0, ((0, 32),))
    route_ids_keys = jax.random.split(jax.random.fold_in(splits[1], 1), TOKENS // TOK_DEV)
    route_ids_turns = jax.random.permutation(jax.random.fold_in(splits[1], 3), TOKENS // TOK_DEV)
    route_ids = jax.vmap(lambda own, number: shared_out(jax.random.fold_in(splits[1], 2), own, number, TOK_DEV, N_ROUTED, TOP, CAP, 2))(route_ids_keys, route_ids_turns).reshape((TOKENS, TOP))
    route_weights = jnp.clip(jnp.exp(math.log(1.0) - 3.912023 * jax.random.uniform(splits[2], (TOKENS, TOP), jnp.float32) ** block_scale(splits[2], (TOKENS, TOP), ((0, 32),), -0.2, 0.2)), 0.02, 1.0)
    hidden = bell_draw(splits[3], (WINDOW, N_DP * N_EXPERT * CAP, F), 1.0, 6.0, ((0, 4), (1, 8)))
    master = bell_draw(splits[4], (F, WINDOW, D), 0.05, 0.3, ((0, 8), (1, 4)), jnp.float32)
    first_moment = bell_draw(splits[5], (F, WINDOW, D), 0.2, 1.2, ((0, 8), (1, 4)), jnp.float32)
    second_moment = jnp.clip(jnp.exp(math.log(0.05) - 3.218876 * jax.random.uniform(splits[6], (F, WINDOW, D), jnp.float32) ** block_scale(splits[6], (F, WINDOW, D), ((0, 8), (1, 4)), -0.2, 0.2)), 0.002, 0.05)
    return dict(cotangent=cotangent, route_ids=route_ids, route_weights=route_weights, hidden=hidden, master=master, first_moment=first_moment, second_moment=second_moment)


beta_one = 0.9
beta_two = 0.999
learning_rate = 0.001
epsilon = 1e-08
decay_rate = 0.1
step_count = 4.0

def slot_table(route_ids, route_weights, window, capacity, local_count, groups):
    tokens = route_ids.shape[0]
    onehot = (route_ids[:, :, None] == jnp.arange(window, dtype=jnp.int32)[None, None, :]).astype(jnp.int32)
    counts = lax.optimization_barrier(jnp.sum(onehot, axis=1))
    before = jnp.cumsum(counts, axis=0) - counts
    ranks = lax.optimization_barrier(jnp.sum(onehot * before[:, None, :], axis=2)).astype(jnp.int32)
    inside = route_ids < window
    position = route_ids % local_count * (groups * capacity) + route_ids // local_count * capacity + ranks
    position = jnp.where(inside, position, window * capacity).astype(jnp.int32)
    anchor = jnp.broadcast_to(jnp.arange(tokens, dtype=jnp.int32)[:, None], route_ids.shape)
    slot_anchor = jnp.zeros((window * capacity + 1,), jnp.int32).at[position.reshape(-1)].set(anchor.reshape(-1))
    masked = jnp.where(inside, route_weights, jnp.zeros_like(route_weights))
    slot_weight = jnp.zeros((window * capacity + 1,), route_weights.dtype).at[position.reshape(-1)].set(masked.reshape(-1))
    return (slot_anchor[:-1], slot_weight[:-1])

def reference(cotangent, route_ids, route_weights, hidden, master, first_moment, second_moment):
    blocks = N_DP * N_EXPERT
    cot_blocks = cotangent.reshape(blocks, TOK_DEV, D)
    id_blocks = route_ids.reshape(blocks, TOK_DEV, TOP)
    weight_blocks = route_weights.reshape(blocks, TOK_DEV, TOP)
    block_index = jnp.arange(blocks, dtype=jnp.int32)

    def accumulate(total, inputs):
        cot_block, id_block, weight_block, number = inputs
        slot_anchor, slot_weight = slot_table(id_block, weight_block, WINDOW, CAP, EXP_DEV, N_EXPERT)
        scaled = (cot_block[slot_anchor].astype(jnp.float32) * slot_weight[:, None]).astype(jnp.bfloat16)
        scaled = scaled.reshape(EXP_DEV, N_EXPERT, CAP, D).transpose(1, 0, 2, 3).reshape(WINDOW, CAP, D)
        start = (number * CAP).astype(jnp.int32)
        hidden_block = lax.dynamic_slice_in_dim(hidden, start, CAP, 1)
        total = total + jnp.einsum('kcf,kcd->kfd', hidden_block.astype(jnp.float32), scaled.astype(jnp.float32))
        return (total, None)
    initial = jnp.zeros((WINDOW, F, D), jnp.float32)
    summed, _ = lax.scan(accumulate, initial, (cot_blocks, id_blocks, weight_blocks, block_index))
    gradient = summed.transpose(1, 0, 2) / jnp.sqrt(jnp.float32(N_EXPERT * CAP))
    new_first = beta_one * first_moment + (1.0 - beta_one) * gradient
    new_second = beta_two * second_moment + (1.0 - beta_two) * gradient * gradient
    corrected_first = new_first / (1.0 - beta_one ** step_count)
    corrected_second = new_second / (1.0 - beta_two ** step_count)
    update = corrected_first / (jnp.sqrt(corrected_second) + epsilon) + decay_rate * master
    new_master = master - learning_rate * update
    return (new_master, new_first, new_second)
```

```python
import functools

import jax
import jax.numpy as jnp
from jax import lax
from jax.experimental import pallas as pl
from jax.experimental.pallas import tpu as pltpu
from jax.sharding import PartitionSpec as P

beta_one = 0.9
beta_two = 0.999
learning_rate = 0.001
epsilon = 1e-08
decay_rate = 0.1
step_count = 4.0

MESH = pl.DeviceIdType.MESH
LANES = 128
CHUNK = 256


def gradient_kernel(
    dp,
    groups,
    ids_ref,
    weights_ref,
    cot_hbm,
    hidden_hbm,
    grad_ref,
    cot,
    hidden,
    turned,
    onehot,
    slot_weight,
    send,
    recv,
    part,
    pair_recv,
    peer_recv,
    own_sum,
    load_sem,
    send_sem,
    recv_sem,
    pair_sem,
    peer_send_sem,
    peer_recv_sem,
):
    d = lax.axis_index("dp")
    s = lax.axis_index("expert")
    half = dp // 2
    parity = lax.rem(d, 2)
    q = d // 2
    partner = d + 1 - 2 * parity
    chunks, width = recv.shape[0], recv.shape[-1]
    local_count, capacity = recv.shape[2], recv.shape[3]
    top, tokens = ids_ref.shape
    rows = groups * capacity
    own = grad_ref.shape[1]
    hidden_units = turned.shape[1]

    load_cot = pltpu.make_async_copy(cot_hbm, cot, load_sem.at[0])
    load_hidden = pltpu.make_async_copy(hidden_hbm, hidden, load_sem.at[1])
    load_cot.start()
    load_hidden.start()

    barrier = pltpu.get_barrier_semaphore()
    for j in range(1, groups):
        pl.semaphore_signal(
            barrier, inc=1, device_id=(d, lax.rem(s + j, groups)), device_id_type=MESH
        )
    pl.semaphore_signal(barrier, inc=1, device_id=(partner, s), device_id_type=MESH)
    for j in range(1, half):
        pl.semaphore_signal(
            barrier,
            inc=1,
            device_id=(lax.rem(q + j, half) * 2 + parity, s),
            device_id_type=MESH,
        )

    window = groups * local_count
    ids = ids_ref[...]
    weights = weights_ref[...]
    lane = lax.broadcasted_iota(jnp.int32, (window, tokens), 1)
    chosen, picked = [], []
    for k in range(window):
        hit = ids == k
        chosen.append(jnp.sum(hit.astype(jnp.int32), axis=0, keepdims=True))
        picked.append(jnp.sum(jnp.where(hit, weights, 0.0), axis=0, keepdims=True))
    count = jnp.concatenate(chosen, axis=0)
    total = count
    shift = 1
    while shift < tokens:
        total = total + jnp.where(lane >= shift, pltpu.roll(total, shift, 1), 0)
        shift *= 2
    rank = jnp.where(count > 0, total - count, -1)
    for k in range(window):
        group, local = k // local_count, k % local_count
        slot = lax.broadcasted_iota(jnp.int32, (capacity, tokens), 0)
        match = slot == rank[k : k + 1, :]
        onehot[group, pl.ds(local * capacity, capacity), :] = jnp.where(match, 1.0, 0.0).astype(
            jnp.bfloat16
        )
        value = jnp.sum(jnp.where(match, picked[k], 0.0), axis=1, keepdims=True)
        slot_weight[group, pl.ds(local * capacity, capacity), :] = jnp.broadcast_to(
            value, (capacity, LANES)
        )

    pl.semaphore_wait(barrier, groups + half - 1)
    load_cot.wait()

    def exchange(c, j):
        return pltpu.make_async_remote_copy(
            src_ref=send.at[c, j - 1],
            dst_ref=recv.at[c, s],
            send_sem=send_sem.at[c, j - 1],
            recv_sem=recv_sem.at[c, j - 1],
            device_id=(d, lax.rem(s + j, groups)),
            device_id_type=MESH,
        )

    def pair(c):
        return pltpu.make_async_remote_copy(
            src_ref=part.at[c, 1 - parity],
            dst_ref=pair_recv.at[c],
            send_sem=pair_sem.at[c, 0],
            recv_sem=pair_sem.at[c, 1],
            device_id=(partner, s),
            device_id_type=MESH,
        )

    def peer(c, j):
        to = lax.rem(q + j, half)
        return pltpu.make_async_remote_copy(
            src_ref=part.at[c, parity, to],
            dst_ref=peer_recv.at[c, j - 1],
            send_sem=peer_send_sem.at[c, j - 1],
            recv_sem=peer_recv_sem.at[c, j - 1],
            device_id=(to * 2 + parity, s),
            device_id_type=MESH,
        )

    order = sorted(range(1, groups), key=lambda j: abs(j - groups / 2)) + [0]

    def dispatch(c, carry):
        columns = cot[:, pl.ds(pl.multiple_of(c * width, width), width)]
        for j in order:
            group = lax.rem(s + j, groups)
            taken = jnp.dot(onehot[group], columns, preferred_element_type=jnp.float32)
            block = (taken * slot_weight[group][:, :1]).astype(jnp.bfloat16)
            block = block.reshape(local_count, capacity, width)
            if j:
                send[c, j - 1] = block
                exchange(c, j).start()
            else:
                recv[c, s] = block
        return carry

    lax.fori_loop(0, chunks, dispatch, 0)

    load_hidden.wait()
    for local in range(local_count):

        def turn(i, carry, local=local):
            at = pl.ds(pl.multiple_of(i * LANES, LANES), LANES)
            turned[local, at, :] = hidden[local, :, at].T
            return carry

        lax.fori_loop(0, hidden_units // LANES, turn, 0)

    def finish(c):
        total = own_sum[...]
        for j in range(1, half):
            peer(c, j).wait_recv()
            total = total + peer_recv[c, j - 1].astype(jnp.float32)
        grad_ref[:, :, pl.ds(pl.multiple_of(c * width, width), width)] = total

    def step(c, carry):
        for j in range(1, groups):
            exchange(c, j).wait_recv()
        for local in range(local_count):
            held = recv[c, :, local].reshape(rows, width)
            product = jnp.dot(turned[local], held, preferred_element_type=jnp.float32)
            for block in range(dp):
                part[c, block % 2, block // 2, local] = product[
                    block * own : (block + 1) * own
                ].astype(jnp.bfloat16)
        pair(c).start()

        @pl.when(c > 0)
        def _():
            finish(c - 1)

        pair(c).wait_recv()
        for j in list(range(1, half)) + [0]:
            to = lax.rem(q + j, half)
            both = part[c, parity, to].astype(jnp.float32) + pair_recv[c, to].astype(jnp.float32)
            if j:
                part[c, parity, to] = both.astype(jnp.bfloat16)
                peer(c, j).start()
            else:
                own_sum[...] = both
        return carry

    lax.fori_loop(0, chunks, step, 0)
    finish(chunks - 1)

    def drain(c, carry):
        for j in range(1, groups):
            exchange(c, j).wait_send()
        pair(c).wait_send()
        for j in range(1, half):
            peer(c, j).wait_send()
        return carry

    lax.fori_loop(0, chunks, drain, 0)


def gradient_sum(dp, groups, cotangent, route_ids, route_weights, hidden, own):
    tokens, depth = cotangent.shape
    local_count, rows, hidden_units = hidden.shape
    capacity = rows // groups
    window = local_count * groups
    chunks = depth // CHUNK
    half = dp // 2
    top = route_ids.shape[1]
    vmem = pl.BlockSpec(memory_space=pltpu.VMEM)
    anywhere = pl.BlockSpec(memory_space=pl.ANY)
    dma = pltpu.SemaphoreType.DMA
    return pl.pallas_call(
        functools.partial(gradient_kernel, dp, groups),
        out_shape=jax.ShapeDtypeStruct((local_count, own, depth), jnp.float32),
        in_specs=[vmem, vmem, anywhere, anywhere],
        out_specs=vmem,
        scratch_shapes=[
            pltpu.VMEM((tokens, depth), jnp.bfloat16),
            pltpu.VMEM(hidden.shape, jnp.bfloat16),
            pltpu.VMEM((local_count, hidden_units, rows), jnp.bfloat16),
            pltpu.VMEM((groups, local_count * capacity, tokens), jnp.bfloat16),
            pltpu.VMEM((groups, local_count * capacity, LANES), jnp.float32),
            pltpu.VMEM((chunks, groups - 1, local_count, capacity, CHUNK), jnp.bfloat16),
            pltpu.VMEM((chunks, groups, local_count, capacity, CHUNK), jnp.bfloat16),
            pltpu.VMEM((chunks, 2, half, local_count, own, CHUNK), jnp.bfloat16),
            pltpu.VMEM((chunks, half, local_count, own, CHUNK), jnp.bfloat16),
            pltpu.VMEM((chunks, half - 1, local_count, own, CHUNK), jnp.bfloat16),
            pltpu.VMEM((local_count, own, CHUNK), jnp.float32),
            dma((2,)),
            dma((chunks, groups - 1)),
            dma((chunks, groups - 1)),
            dma((chunks, 2)),
            dma((chunks, half - 1)),
            dma((chunks, half - 1)),
        ],
        compiler_params=pltpu.CompilerParams(
            collective_id=0, has_side_effects=True, vmem_limit_bytes=64 * 1024 * 1024 - 65536
        ),
    )(route_ids.T, route_weights.T, cotangent, hidden)


def solution(mesh):
    dp, groups = mesh.shape["dp"], mesh.shape["expert"]

    def shards(cotangent, route_ids, route_weights, hidden, master, first_moment, second_moment):
        capacity = hidden.shape[1] // groups
        summed = gradient_sum(
            dp, groups, cotangent, route_ids, route_weights, hidden, master.shape[0]
        )
        gradient = summed.transpose(1, 0, 2) / jnp.sqrt(jnp.float32(groups * capacity))
        new_first = beta_one * first_moment + (1.0 - beta_one) * gradient
        new_second = beta_two * second_moment + (1.0 - beta_two) * gradient * gradient
        corrected_first = new_first / (1.0 - beta_one**step_count)
        corrected_second = new_second / (1.0 - beta_two**step_count)
        update = corrected_first / (jnp.sqrt(corrected_second) + epsilon) + decay_rate * master
        new_master = master - learning_rate * update
        return (new_master, new_first, new_second)

    placed = (
        P(("dp", "expert"), None),
        P(("dp", "expert"), None),
        P(("dp", "expert"), None),
        P("expert", "dp", None),
        P("dp", "expert", None),
        P("dp", "expert", None),
        P("dp", "expert", None),
    )
    return jax.shard_map(
        shards,
        mesh=mesh,
        in_specs=placed,
        out_specs=(P("dp", "expert", None), P("dp", "expert", None), P("dp", "expert", None)),
        check_vma=False,
    )
```

```python
import functools

import jax
import jax.numpy as jnp
from jax import lax
from jax.experimental import pallas as pl
from jax.experimental.pallas import tpu as pltpu
from jax.sharding import PartitionSpec as P

beta_one = 0.9
beta_two = 0.999
learning_rate = 0.001
epsilon = 1e-08
decay_rate = 0.1
step_count = 4.0

MESH = pl.DeviceIdType.MESH
LANES = 128
CHUNK = 128


def gradient_kernel(
    dp,
    groups,
    ids_ref,
    weights_ref,
    cot_hbm,
    hidden_hbm,
    grad_ref,
    cot,
    hidden,
    turned,
    onehot,
    slot_weight,
    send,
    recv,
    part,
    pair_recv,
    peer_recv,
    own_sum,
    load_sem,
    send_sem,
    recv_sem,
    pair_sem,
    peer_send_sem,
    peer_recv_sem,
):
    d = lax.axis_index("dp")
    s = lax.axis_index("expert")
    half = dp // 2
    parity = lax.rem(d, 2)
    q = d // 2
    partner = d + 1 - 2 * parity
    chunks, width = recv.shape[0], recv.shape[-1]
    local_count, capacity = recv.shape[2], recv.shape[3]
    top, tokens = ids_ref.shape
    rows = groups * capacity
    own = own_sum.shape[1]
    stride = chunks * (width // LANES) * local_count
    hidden_units = turned.shape[1]

    load_cot = pltpu.make_async_copy(cot_hbm, cot, load_sem.at[0])
    load_hidden = pltpu.make_async_copy(hidden_hbm, hidden, load_sem.at[1])
    load_cot.start()
    load_hidden.start()

    barrier = pltpu.get_barrier_semaphore()
    for j in range(1, groups):
        pl.semaphore_signal(
            barrier, inc=1, device_id=(d, lax.rem(s + j, groups)), device_id_type=MESH
        )
    pl.semaphore_signal(barrier, inc=1, device_id=(partner, s), device_id_type=MESH)
    for j in range(1, half):
        pl.semaphore_signal(
            barrier,
            inc=1,
            device_id=(lax.rem(q + j, half) * 2 + parity, s),
            device_id_type=MESH,
        )

    window = groups * local_count
    ids = ids_ref[...]
    weights = weights_ref[...]
    lane = lax.broadcasted_iota(jnp.int32, (window, tokens), 1)
    chosen, picked = [], []
    for k in range(window):
        hit = ids == k
        chosen.append(jnp.sum(hit.astype(jnp.int32), axis=0, keepdims=True))
        picked.append(jnp.sum(jnp.where(hit, weights, 0.0), axis=0, keepdims=True))
    count = jnp.concatenate(chosen, axis=0)
    total = count
    shift = 1
    while shift < tokens:
        total = total + jnp.where(lane >= shift, pltpu.roll(total, shift, 1), 0)
        shift *= 2
    rank = jnp.where(count > 0, total - count, -1)
    for k in range(window):
        group, local = k // local_count, k % local_count
        slot = lax.broadcasted_iota(jnp.int32, (capacity, tokens), 0)
        match = slot == rank[k : k + 1, :]
        onehot[group, pl.ds(local * capacity, capacity), :] = jnp.where(match, 1.0, 0.0).astype(
            jnp.bfloat16
        )
        value = jnp.sum(jnp.where(match, picked[k], 0.0), axis=1, keepdims=True)
        slot_weight[group, pl.ds(local * capacity, capacity), :] = jnp.broadcast_to(
            value, (capacity, LANES)
        )

    pl.semaphore_wait(barrier, groups + half - 1)
    load_cot.wait()

    def exchange(c, j):
        return pltpu.make_async_remote_copy(
            src_ref=send.at[c, j - 1],
            dst_ref=recv.at[c, s],
            send_sem=send_sem.at[c, j - 1],
            recv_sem=recv_sem.at[c, j - 1],
            device_id=(d, lax.rem(s + j, groups)),
            device_id_type=MESH,
        )

    def pair(c):
        return pltpu.make_async_remote_copy(
            src_ref=part.at[lax.rem(c, 2), 1 - parity],
            dst_ref=pair_recv.at[lax.rem(c, 2)],
            send_sem=pair_sem.at[c, 0],
            recv_sem=pair_sem.at[c, 1],
            device_id=(partner, s),
            device_id_type=MESH,
        )

    def peer(c, j):
        to = lax.rem(q + j, half)
        return pltpu.make_async_remote_copy(
            src_ref=part.at[lax.rem(c, 2), parity, to],
            dst_ref=peer_recv.at[lax.rem(c, 2), j - 1],
            send_sem=peer_send_sem.at[c, j - 1],
            recv_sem=peer_recv_sem.at[c, j - 1],
            device_id=(to * 2 + parity, s),
            device_id_type=MESH,
        )

    order = sorted(range(1, groups), key=lambda j: abs(j - groups / 2)) + [0]

    def dispatch(c, carry):
        columns = cot[:, pl.ds(pl.multiple_of(c * width, width), width)]
        for j in order:
            group = lax.rem(s + j, groups)
            taken = jnp.dot(onehot[group], columns, preferred_element_type=jnp.float32)
            block = (taken * slot_weight[group][:, :1]).astype(jnp.bfloat16)
            block = block.reshape(local_count, capacity, width)
            if j:
                send[c, j - 1] = block
                exchange(c, j).start()
            else:
                recv[c, s] = block
        return carry

    lax.fori_loop(0, chunks, dispatch, 0)

    load_hidden.wait()
    for local in range(local_count):

        def turn(i, carry, local=local):
            at = pl.ds(pl.multiple_of(i * LANES, LANES), LANES)
            turned[local, at, :] = hidden[local, :, at].T
            return carry

        lax.fori_loop(0, hidden_units // LANES, turn, 0)

    def finish(c):
        total = own_sum[...]
        for j in range(1, half):
            peer(c, j).wait_recv()
            total = total + peer_recv[lax.rem(c, 2), j - 1].astype(jnp.float32)
        for local in range(local_count):
            for tile in range(width // LANES):
                first = (c * (width // LANES) + tile) * local_count + local
                grad_ref[pl.ds(first, own, stride=stride), :] = total[
                    local, :, tile * LANES : (tile + 1) * LANES
                ]

    def sent(c):
        pair(c).wait_send()
        for j in range(1, half):
            peer(c, j).wait_send()

    def step(c, carry):
        slot = lax.rem(c, 2)

        @pl.when(c > 1)
        def _():
            sent(c - 2)

        for j in range(1, groups):
            exchange(c, j).wait_recv()
        for local in range(local_count):
            held = recv[c, :, local].reshape(rows, width)
            product = jnp.dot(turned[local], held, preferred_element_type=jnp.float32)
            for block in range(dp):
                part[slot, block % 2, block // 2, local] = product[
                    block * own : (block + 1) * own
                ].astype(jnp.bfloat16)
        pair(c).start()

        @pl.when(c > 0)
        def _():
            finish(c - 1)

        pair(c).wait_recv()
        for j in list(range(1, half)) + [0]:
            to = lax.rem(q + j, half)
            both = part[slot, parity, to].astype(jnp.float32) + pair_recv[slot, to].astype(jnp.float32)
            if j:
                part[slot, parity, to] = both.astype(jnp.bfloat16)
                peer(c, j).start()
            else:
                own_sum[...] = both
        return carry

    lax.fori_loop(0, chunks, step, 0)
    finish(chunks - 1)

    def drain(c, carry):
        for j in range(1, groups):
            exchange(c, j).wait_send()
        return carry

    for c in range(max(chunks - 2, 0), chunks):
        sent(c)
    lax.fori_loop(0, chunks, drain, 0)


def gradient_sum(dp, groups, cotangent, route_ids, route_weights, hidden, own):
    tokens, depth = cotangent.shape
    local_count, rows, hidden_units = hidden.shape
    capacity = rows // groups
    window = local_count * groups
    chunks = depth // CHUNK
    half = dp // 2
    top = route_ids.shape[1]
    vmem = pl.BlockSpec(memory_space=pltpu.VMEM)
    anywhere = pl.BlockSpec(memory_space=pltpu.HBM)
    dma = pltpu.SemaphoreType.DMA
    return pl.pallas_call(
        functools.partial(gradient_kernel, dp, groups),
        out_shape=jax.ShapeDtypeStruct((own * depth * local_count // LANES, LANES), jnp.float32),
        in_specs=[vmem, vmem, anywhere, anywhere],
        out_specs=vmem,
        scratch_shapes=[
            pltpu.VMEM((tokens, depth), jnp.bfloat16),
            pltpu.VMEM(hidden.shape, jnp.bfloat16),
            pltpu.VMEM((local_count, hidden_units, rows), jnp.bfloat16),
            pltpu.VMEM((groups, local_count * capacity, tokens), jnp.bfloat16),
            pltpu.VMEM((groups, local_count * capacity, LANES), jnp.float32),
            pltpu.VMEM((chunks, groups - 1, local_count, capacity, CHUNK), jnp.bfloat16),
            pltpu.VMEM((chunks, groups, local_count, capacity, CHUNK), jnp.bfloat16),
            pltpu.VMEM((2, 2, half, local_count, own, CHUNK), jnp.bfloat16),
            pltpu.VMEM((2, half, local_count, own, CHUNK), jnp.bfloat16),
            pltpu.VMEM((2, half - 1, local_count, own, CHUNK), jnp.bfloat16),
            pltpu.VMEM((local_count, own, CHUNK), jnp.float32),
            dma((2,)),
            dma((chunks, groups - 1)),
            dma((chunks, groups - 1)),
            dma((chunks, 2)),
            dma((chunks, half - 1)),
            dma((chunks, half - 1)),
        ],
        compiler_params=pltpu.CompilerParams(
            collective_id=0, has_side_effects=True, vmem_limit_bytes=44 * 1024 * 1024
        ),
    )(route_ids.T, route_weights.T, cotangent, hidden)


def solution(mesh):
    dp, groups = mesh.shape["dp"], mesh.shape["expert"]

    def shards(cotangent, route_ids, route_weights, hidden, master, first_moment, second_moment):
        capacity = hidden.shape[1] // groups
        summed = gradient_sum(
            dp, groups, cotangent, route_ids, route_weights, hidden, master.shape[0]
        )
        shape = master.shape
        split = (shape[0], shape[1], shape[2] // LANES, LANES)

        def flat(x):
            return x.reshape(split).transpose(0, 2, 1, 3).reshape(-1, LANES)

        def whole(x):
            return x.reshape(split[0], split[2], split[1], LANES).transpose(0, 2, 1, 3).reshape(shape)

        master, first_moment, second_moment = lax.optimization_barrier(
            (flat(master), flat(first_moment), flat(second_moment))
        )
        gradient = summed / jnp.sqrt(jnp.float32(groups * capacity))
        new_first = beta_one * first_moment + (1.0 - beta_one) * gradient
        new_second = beta_two * second_moment + (1.0 - beta_two) * gradient * gradient
        corrected_first = new_first / (1.0 - beta_one**step_count)
        corrected_second = new_second / (1.0 - beta_two**step_count)
        update = corrected_first / (jnp.sqrt(corrected_second) + epsilon) + decay_rate * master
        new_master = master - learning_rate * update
        return (whole(new_master), whole(new_first), whole(new_second))

    placed = (
        P(("dp", "expert"), None),
        P(("dp", "expert"), None),
        P(("dp", "expert"), None),
        P("expert", "dp", None),
        P("dp", "expert", None),
        P("dp", "expert", None),
        P("dp", "expert", None),
    )
    return jax.shard_map(
        shards,
        mesh=mesh,
        in_specs=placed,
        out_specs=(P("dp", "expert", None), P("dp", "expert", None), P("dp", "expert", None)),
        check_vma=False,
    )
```

```python
import functools

import jax
import jax.numpy as jnp
from jax import lax
from jax.experimental import pallas as pl
from jax.experimental.pallas import tpu as pltpu
from jax.sharding import PartitionSpec as P

beta_one = 0.9
beta_two = 0.999
learning_rate = 0.001
epsilon = 1e-08
decay_rate = 0.1
step_count = 4.0

MESH = pl.DeviceIdType.MESH
LANES = 128
CHUNK = 128
SLOTS = 4


def gradient_kernel(
    dp,
    groups,
    ids_ref,
    weights_ref,
    cot_hbm,
    hidden_hbm,
    grad_ref,
    cot,
    hidden,
    turned,
    onehot,
    slot_weight,
    send,
    recv,
    part,
    pair_recv,
    peer_recv,
    own_sum,
    load_sem,
    send_sem,
    recv_sem,
    pair_sem,
    peer_send_sem,
    peer_recv_sem,
):
    d = lax.axis_index("dp")
    s = lax.axis_index("expert")
    half = dp // 2
    parity = lax.rem(d, 2)
    q = d // 2
    partner = d + 1 - 2 * parity
    chunks, width = recv.shape[0], recv.shape[-1]
    local_count, capacity = recv.shape[2], recv.shape[3]
    top, tokens = ids_ref.shape
    rows = groups * capacity
    own = own_sum.shape[2]
    stride = chunks * (width // LANES) * local_count
    hidden_units = turned.shape[1]

    load_cot = pltpu.make_async_copy(cot_hbm, cot, load_sem.at[0])
    load_hidden = pltpu.make_async_copy(hidden_hbm, hidden, load_sem.at[1])
    load_cot.start()
    load_hidden.start()

    barrier = pltpu.get_barrier_semaphore()
    for j in range(1, groups):
        pl.semaphore_signal(
            barrier, inc=1, device_id=(d, lax.rem(s + j, groups)), device_id_type=MESH
        )
    pl.semaphore_signal(barrier, inc=1, device_id=(partner, s), device_id_type=MESH)
    for j in range(1, half):
        pl.semaphore_signal(
            barrier,
            inc=1,
            device_id=(lax.rem(q + j, half) * 2 + parity, s),
            device_id_type=MESH,
        )

    window = groups * local_count
    ids = ids_ref[...]
    weights = weights_ref[...]
    lane = lax.broadcasted_iota(jnp.int32, (window, tokens), 1)
    chosen, picked = [], []
    for k in range(window):
        hit = ids == k
        chosen.append(jnp.sum(hit.astype(jnp.int32), axis=0, keepdims=True))
        picked.append(jnp.sum(jnp.where(hit, weights, 0.0), axis=0, keepdims=True))
    count = jnp.concatenate(chosen, axis=0)
    total = count
    shift = 1
    while shift < tokens:
        total = total + jnp.where(lane >= shift, pltpu.roll(total, shift, 1), 0)
        shift *= 2
    rank = jnp.where(count > 0, total - count, -1)
    for k in range(window):
        group, local = k // local_count, k % local_count
        slot = lax.broadcasted_iota(jnp.int32, (capacity, tokens), 0)
        match = slot == rank[k : k + 1, :]
        onehot[group, pl.ds(local * capacity, capacity), :] = jnp.where(match, 1.0, 0.0).astype(
            jnp.bfloat16
        )
        value = jnp.sum(jnp.where(match, picked[k], 0.0), axis=1, keepdims=True)
        slot_weight[group, pl.ds(local * capacity, capacity), :] = jnp.broadcast_to(
            value, (capacity, LANES)
        )

    pl.semaphore_wait(barrier, groups + half - 1)
    load_cot.wait()

    def exchange(c, j):
        return pltpu.make_async_remote_copy(
            src_ref=send.at[c, j - 1],
            dst_ref=recv.at[c, s],
            send_sem=send_sem.at[c, j - 1],
            recv_sem=recv_sem.at[c, j - 1],
            device_id=(d, lax.rem(s + j, groups)),
            device_id_type=MESH,
        )

    def pair(c):
        return pltpu.make_async_remote_copy(
            src_ref=part.at[lax.rem(c, SLOTS), 1 - parity],
            dst_ref=pair_recv.at[lax.rem(c, SLOTS)],
            send_sem=pair_sem.at[c, 0],
            recv_sem=pair_sem.at[c, 1],
            device_id=(partner, s),
            device_id_type=MESH,
        )

    def peer(c, j):
        to = lax.rem(q + j, half)
        return pltpu.make_async_remote_copy(
            src_ref=part.at[lax.rem(c, SLOTS), parity, to],
            dst_ref=peer_recv.at[lax.rem(c, SLOTS), j - 1],
            send_sem=peer_send_sem.at[c, j - 1],
            recv_sem=peer_recv_sem.at[c, j - 1],
            device_id=(to * 2 + parity, s),
            device_id_type=MESH,
        )

    order = sorted(range(1, groups), key=lambda j: abs(j - groups / 2)) + [0]

    def dispatch(c, carry):
        columns = cot[:, pl.ds(pl.multiple_of(c * width, width), width)]
        for j in order:
            group = lax.rem(s + j, groups)
            taken = jnp.dot(onehot[group], columns, preferred_element_type=jnp.float32)
            block = (taken * slot_weight[group][:, :1]).astype(jnp.bfloat16)
            block = block.reshape(local_count, capacity, width)
            if j:
                send[c, j - 1] = block
                exchange(c, j).start()
            else:
                recv[c, s] = block
        return carry

    lax.fori_loop(0, chunks, dispatch, 0)

    load_hidden.wait()
    for local in range(local_count):

        def turn(i, carry, local=local):
            at = pl.ds(pl.multiple_of(i * LANES, LANES), LANES)
            turned[local, at, :] = hidden[local, :, at].T
            return carry

        lax.fori_loop(0, hidden_units // LANES, turn, 0)

    def finish(c):
        total = own_sum[lax.rem(c, SLOTS)]
        for j in range(1, half):
            peer(c, j).wait_recv()
            total = total + peer_recv[lax.rem(c, SLOTS), j - 1].astype(jnp.float32)
        for local in range(local_count):
            for tile in range(width // LANES):
                first = (c * (width // LANES) + tile) * local_count + local
                grad_ref[pl.ds(first, own, stride=stride), :] = total[
                    local, :, tile * LANES : (tile + 1) * LANES
                ]

    def combine(c):
        slot = lax.rem(c, SLOTS)
        pair(c).wait_recv()
        for j in list(range(1, half)) + [0]:
            to = lax.rem(q + j, half)
            both = part[slot, parity, to].astype(jnp.float32) + pair_recv[slot, to].astype(
                jnp.float32
            )
            if j:
                part[slot, parity, to] = both.astype(jnp.bfloat16)
                peer(c, j).start()
            else:
                own_sum[slot] = both

    def sent(c):
        pair(c).wait_send()
        for j in range(1, half):
            peer(c, j).wait_send()

    def step(c, carry):
        slot = lax.rem(c, SLOTS)

        @pl.when(c >= SLOTS)
        def _():
            sent(c - SLOTS)

        for j in range(1, groups):
            exchange(c, j).wait_recv()
        for local in range(local_count):
            held = recv[c, :, local].reshape(rows, width)
            product = jnp.dot(turned[local], held, preferred_element_type=jnp.float32)
            for block in range(dp):
                part[slot, block % 2, block // 2, local] = product[
                    block * own : (block + 1) * own
                ].astype(jnp.bfloat16)
        pair(c).start()

        @pl.when(c > 0)
        def _():
            combine(c - 1)

        @pl.when(c > 1)
        def _():
            finish(c - 2)

        return carry

    lax.fori_loop(0, chunks, step, 0)
    combine(chunks - 1)
    if chunks > 1:
        finish(chunks - 2)
    finish(chunks - 1)

    def drain(c, carry):
        for j in range(1, groups):
            exchange(c, j).wait_send()
        return carry

    for c in range(max(chunks - SLOTS, 0), chunks):
        sent(c)
    lax.fori_loop(0, chunks, drain, 0)


def gradient_sum(dp, groups, cotangent, route_ids, route_weights, hidden, own):
    tokens, depth = cotangent.shape
    local_count, rows, hidden_units = hidden.shape
    capacity = rows // groups
    window = local_count * groups
    chunks = depth // CHUNK
    half = dp // 2
    top = route_ids.shape[1]
    vmem = pl.BlockSpec(memory_space=pltpu.VMEM)
    anywhere = pl.BlockSpec(memory_space=pltpu.HBM)
    dma = pltpu.SemaphoreType.DMA
    return pl.pallas_call(
        functools.partial(gradient_kernel, dp, groups),
        out_shape=jax.ShapeDtypeStruct((own * depth * local_count // LANES, LANES), jnp.float32),
        in_specs=[vmem, vmem, anywhere, anywhere],
        out_specs=vmem,
        scratch_shapes=[
            pltpu.VMEM((tokens, depth), jnp.bfloat16),
            pltpu.VMEM(hidden.shape, jnp.bfloat16),
            pltpu.VMEM((local_count, hidden_units, rows), jnp.bfloat16),
            pltpu.VMEM((groups, local_count * capacity, tokens), jnp.bfloat16),
            pltpu.VMEM((groups, local_count * capacity, LANES), jnp.float32),
            pltpu.VMEM((chunks, groups - 1, local_count, capacity, CHUNK), jnp.bfloat16),
            pltpu.VMEM((chunks, groups, local_count, capacity, CHUNK), jnp.bfloat16),
            pltpu.VMEM((SLOTS, 2, half, local_count, own, CHUNK), jnp.bfloat16),
            pltpu.VMEM((SLOTS, half, local_count, own, CHUNK), jnp.bfloat16),
            pltpu.VMEM((SLOTS, half - 1, local_count, own, CHUNK), jnp.bfloat16),
            pltpu.VMEM((SLOTS, local_count, own, CHUNK), jnp.float32),
            dma((2,)),
            dma((chunks, groups - 1)),
            dma((chunks, groups - 1)),
            dma((chunks, 2)),
            dma((chunks, half - 1)),
            dma((chunks, half - 1)),
        ],
        compiler_params=pltpu.CompilerParams(
            collective_id=0, has_side_effects=True, vmem_limit_bytes=50 * 1024 * 1024
        ),
    )(route_ids.T, route_weights.T, cotangent, hidden)


def solution(mesh):
    dp, groups = mesh.shape["dp"], mesh.shape["expert"]

    def shards(cotangent, route_ids, route_weights, hidden, master, first_moment, second_moment):
        capacity = hidden.shape[1] // groups
        summed = gradient_sum(
            dp, groups, cotangent, route_ids, route_weights, hidden, master.shape[0]
        )
        shape = master.shape
        split = (shape[0], shape[1], shape[2] // LANES, LANES)

        def flat(x):
            return x.reshape(split).transpose(0, 2, 1, 3).reshape(-1, LANES)

        def whole(x):
            return x.reshape(split[0], split[2], split[1], LANES).transpose(0, 2, 1, 3).reshape(shape)

        master, first_moment, second_moment = lax.optimization_barrier(
            (flat(master), flat(first_moment), flat(second_moment))
        )
        gradient = summed / jnp.sqrt(jnp.float32(groups * capacity))
        new_first = beta_one * first_moment + (1.0 - beta_one) * gradient
        new_second = beta_two * second_moment + (1.0 - beta_two) * gradient * gradient
        corrected_first = new_first / (1.0 - beta_one**step_count)
        corrected_second = new_second / (1.0 - beta_two**step_count)
        update = corrected_first / (jnp.sqrt(corrected_second) + epsilon) + decay_rate * master
        new_master = master - learning_rate * update
        return (whole(new_master), whole(new_first), whole(new_second))

    placed = (
        P(("dp", "expert"), None),
        P(("dp", "expert"), None),
        P(("dp", "expert"), None),
        P("expert", "dp", None),
        P("dp", "expert", None),
        P("dp", "expert", None),
        P("dp", "expert", None),
    )
    return jax.shard_map(
        shards,
        mesh=mesh,
        in_specs=placed,
        out_specs=(P("dp", "expert", None), P("dp", "expert", None), P("dp", "expert", None)),
        check_vma=False,
    )
```

```python
import functools

import jax
import jax.numpy as jnp
from jax import lax
from jax.experimental import pallas as pl
from jax.experimental.pallas import tpu as pltpu
from jax.sharding import PartitionSpec as P

beta_one = 0.9
beta_two = 0.999
learning_rate = 0.001
epsilon = 1e-08
decay_rate = 0.1
step_count = 4.0

MESH = pl.DeviceIdType.MESH
LANES = 128
CHUNK = 128
SLOTS = 4


def gradient_kernel(
    dp,
    groups,
    ids_ref,
    weights_ref,
    cot_hbm,
    hidden_hbm,
    grad_ref,
    cot,
    hidden,
    turned,
    onehot,
    slot_weight,
    send,
    recv,
    part,
    pair_recv,
    peer_recv,
    own_sum,
    load_sem,
    send_sem,
    recv_sem,
    pair_sem,
    peer_send_sem,
    peer_recv_sem,
):
    d = lax.axis_index("dp")
    s = lax.axis_index("expert")
    half = dp // 2
    parity = lax.rem(d, 2)
    q = d // 2
    partner = d + 1 - 2 * parity
    chunks, width = recv.shape[0], recv.shape[-1]
    local_count, capacity = recv.shape[2], recv.shape[3]
    top, tokens = ids_ref.shape
    rows = groups * capacity
    own = own_sum.shape[2]
    stride = chunks * (width // LANES) * local_count
    hidden_units = turned.shape[1]

    load_cot = pltpu.make_async_copy(cot_hbm, cot, load_sem.at[0])
    load_hidden = pltpu.make_async_copy(hidden_hbm, hidden, load_sem.at[1])
    load_cot.start()
    load_hidden.start()

    barrier = pltpu.get_barrier_semaphore()
    for j in range(1, groups):
        pl.semaphore_signal(
            barrier, inc=1, device_id=(d, lax.rem(s + j, groups)), device_id_type=MESH
        )
    pl.semaphore_signal(barrier, inc=1, device_id=(partner, s), device_id_type=MESH)
    for j in range(1, half):
        pl.semaphore_signal(
            barrier,
            inc=1,
            device_id=(lax.rem(q + j, half) * 2 + parity, s),
            device_id_type=MESH,
        )

    window = groups * local_count
    ids = ids_ref[...]
    weights = weights_ref[...]
    lane = lax.broadcasted_iota(jnp.int32, (window, tokens), 1)
    chosen, picked = [], []
    for k in range(window):
        hit = ids == k
        chosen.append(jnp.sum(hit.astype(jnp.int32), axis=0, keepdims=True))
        picked.append(jnp.sum(jnp.where(hit, weights, 0.0), axis=0, keepdims=True))
    count = jnp.concatenate(chosen, axis=0)
    total = count
    shift = 1
    while shift < tokens:
        total = total + jnp.where(lane >= shift, pltpu.roll(total, shift, 1), 0)
        shift *= 2
    rank = jnp.where(count > 0, total - count, -1)
    for k in range(window):
        group, local = k // local_count, k % local_count
        slot = lax.broadcasted_iota(jnp.int32, (capacity, tokens), 0)
        match = slot == rank[k : k + 1, :]
        onehot[group, pl.ds(local * capacity, capacity), :] = jnp.where(match, 1.0, 0.0).astype(
            jnp.bfloat16
        )
        value = jnp.sum(jnp.where(match, picked[k], 0.0), axis=1, keepdims=True)
        slot_weight[group, pl.ds(local * capacity, capacity), :] = jnp.broadcast_to(
            value, (capacity, LANES)
        )

    pl.semaphore_wait(barrier, groups + half - 1)
    load_cot.wait()

    def exchange(c, j):
        return pltpu.make_async_remote_copy(
            src_ref=send.at[c, j - 1],
            dst_ref=recv.at[c, s],
            send_sem=send_sem.at[c, j - 1],
            recv_sem=recv_sem.at[c, j - 1],
            device_id=(d, lax.rem(s + j, groups)),
            device_id_type=MESH,
        )

    def pair(c):
        return pltpu.make_async_remote_copy(
            src_ref=part.at[lax.rem(c, SLOTS), 1 - parity],
            dst_ref=pair_recv.at[lax.rem(c, SLOTS)],
            send_sem=pair_sem.at[c, 0],
            recv_sem=pair_sem.at[c, 1],
            device_id=(partner, s),
            device_id_type=MESH,
        )

    def peer(c, j):
        to = lax.rem(q + j, half)
        return pltpu.make_async_remote_copy(
            src_ref=part.at[lax.rem(c, SLOTS), parity, to],
            dst_ref=peer_recv.at[lax.rem(c, SLOTS), j - 1],
            send_sem=peer_send_sem.at[c, j - 1],
            recv_sem=peer_recv_sem.at[c, j - 1],
            device_id=(to * 2 + parity, s),
            device_id_type=MESH,
        )

    upper = s * 2 // groups
    late = list(range(1, groups))
    early = late[1:2] + late[:1] + late[2:]
    order = []
    for first, second in zip(early, late):
        j = first + (second - first) * parity
        order.append(j + (groups - 2 * j) * upper)

    def dispatch(c, carry):
        columns = cot[:, pl.ds(pl.multiple_of(c * width, width), width)]
        for j in order + [None]:
            group = s if j is None else lax.rem(s + j, groups)
            taken = jnp.dot(onehot[group], columns, preferred_element_type=jnp.float32)
            block = (taken * slot_weight[group][:, :1]).astype(jnp.bfloat16)
            block = block.reshape(local_count, capacity, width)
            if j is None:
                recv[c, s] = block
            else:
                send[c, j - 1] = block
                exchange(c, j).start()
        return carry

    lax.fori_loop(0, chunks, dispatch, 0)

    load_hidden.wait()
    for local in range(local_count):

        def turn(i, carry, local=local):
            at = pl.ds(pl.multiple_of(i * LANES, LANES), LANES)
            turned[local, at, :] = hidden[local, :, at].T
            return carry

        lax.fori_loop(0, hidden_units // LANES, turn, 0)

    def finish(c):
        total = own_sum[lax.rem(c, SLOTS)]
        for j in range(1, half):
            peer(c, j).wait_recv()
            total = total + peer_recv[lax.rem(c, SLOTS), j - 1].astype(jnp.float32)
        for local in range(local_count):
            for tile in range(width // LANES):
                first = (c * (width // LANES) + tile) * local_count + local
                grad_ref[pl.ds(first, own, stride=stride), :] = total[
                    local, :, tile * LANES : (tile + 1) * LANES
                ]

    def combine(c):
        slot = lax.rem(c, SLOTS)
        pair(c).wait_recv()
        for j in list(range(1, half)) + [0]:
            to = lax.rem(q + j, half)
            both = part[slot, parity, to].astype(jnp.float32) + pair_recv[slot, to].astype(
                jnp.float32
            )
            if j:
                part[slot, parity, to] = both.astype(jnp.bfloat16)
                peer(c, j).start()
            else:
                own_sum[slot] = both

    def sent(c):
        pair(c).wait_send()
        for j in range(1, half):
            peer(c, j).wait_send()

    def step(c, carry):
        slot = lax.rem(c, SLOTS)

        @pl.when(c >= SLOTS)
        def _():
            sent(c - SLOTS)

        for j in range(1, groups):
            exchange(c, j).wait_recv()
        for local in range(local_count):
            held = recv[c, :, local].reshape(rows, width)
            product = jnp.dot(turned[local], held, preferred_element_type=jnp.float32)
            for block in range(dp):
                part[slot, block % 2, block // 2, local] = product[
                    block * own : (block + 1) * own
                ].astype(jnp.bfloat16)
        pair(c).start()

        @pl.when(c > 0)
        def _():
            combine(c - 1)

        @pl.when(c > 1)
        def _():
            finish(c - 2)

        return carry

    lax.fori_loop(0, chunks, step, 0)
    combine(chunks - 1)
    if chunks > 1:
        finish(chunks - 2)
    finish(chunks - 1)

    def drain(c, carry):
        for j in range(1, groups):
            exchange(c, j).wait_send()
        return carry

    for c in range(max(chunks - SLOTS, 0), chunks):
        sent(c)
    lax.fori_loop(0, chunks, drain, 0)


def gradient_sum(dp, groups, cotangent, route_ids, route_weights, hidden, own):
    tokens, depth = cotangent.shape
    local_count, rows, hidden_units = hidden.shape
    capacity = rows // groups
    window = local_count * groups
    chunks = depth // CHUNK
    half = dp // 2
    top = route_ids.shape[1]
    vmem = pl.BlockSpec(memory_space=pltpu.VMEM)
    anywhere = pl.BlockSpec(memory_space=pltpu.HBM)
    dma = pltpu.SemaphoreType.DMA
    return pl.pallas_call(
        functools.partial(gradient_kernel, dp, groups),
        out_shape=jax.ShapeDtypeStruct((own * depth * local_count // LANES, LANES), jnp.float32),
        in_specs=[vmem, vmem, anywhere, anywhere],
        out_specs=vmem,
        scratch_shapes=[
            pltpu.VMEM((tokens, depth), jnp.bfloat16),
            pltpu.VMEM(hidden.shape, jnp.bfloat16),
            pltpu.VMEM((local_count, hidden_units, rows), jnp.bfloat16),
            pltpu.VMEM((groups, local_count * capacity, tokens), jnp.bfloat16),
            pltpu.VMEM((groups, local_count * capacity, LANES), jnp.float32),
            pltpu.VMEM((chunks, groups - 1, local_count, capacity, CHUNK), jnp.bfloat16),
            pltpu.VMEM((chunks, groups, local_count, capacity, CHUNK), jnp.bfloat16),
            pltpu.VMEM((SLOTS, 2, half, local_count, own, CHUNK), jnp.bfloat16),
            pltpu.VMEM((SLOTS, half, local_count, own, CHUNK), jnp.bfloat16),
            pltpu.VMEM((SLOTS, half - 1, local_count, own, CHUNK), jnp.bfloat16),
            pltpu.VMEM((SLOTS, local_count, own, CHUNK), jnp.float32),
            dma((2,)),
            dma((chunks, groups - 1)),
            dma((chunks, groups - 1)),
            dma((chunks, 2)),
            dma((chunks, half - 1)),
            dma((chunks, half - 1)),
        ],
        compiler_params=pltpu.CompilerParams(
            collective_id=0, has_side_effects=True, vmem_limit_bytes=50 * 1024 * 1024
        ),
    )(route_ids.T, route_weights.T, cotangent, hidden)


def solution(mesh):
    dp, groups = mesh.shape["dp"], mesh.shape["expert"]

    def shards(cotangent, route_ids, route_weights, hidden, master, first_moment, second_moment):
        capacity = hidden.shape[1] // groups
        summed = gradient_sum(
            dp, groups, cotangent, route_ids, route_weights, hidden, master.shape[0]
        )
        shape = master.shape
        split = (shape[0], shape[1], shape[2] // LANES, LANES)

        def flat(x):
            return x.reshape(split).transpose(0, 2, 1, 3).reshape(-1, LANES)

        def whole(x):
            return x.reshape(split[0], split[2], split[1], LANES).transpose(0, 2, 1, 3).reshape(shape)

        master, first_moment, second_moment = lax.optimization_barrier(
            (flat(master), flat(first_moment), flat(second_moment))
        )
        gradient = summed / jnp.sqrt(jnp.float32(groups * capacity))
        new_first = beta_one * first_moment + (1.0 - beta_one) * gradient
        new_second = beta_two * second_moment + (1.0 - beta_two) * gradient * gradient
        corrected_first = new_first / (1.0 - beta_one**step_count)
        corrected_second = new_second / (1.0 - beta_two**step_count)
        update = corrected_first / (jnp.sqrt(corrected_second) + epsilon) + decay_rate * master
        new_master = master - learning_rate * update
        return (whole(new_master), whole(new_first), whole(new_second))

    placed = (
        P(("dp", "expert"), None),
        P(("dp", "expert"), None),
        P(("dp", "expert"), None),
        P("expert", "dp", None),
        P("dp", "expert", None),
        P("dp", "expert", None),
        P("dp", "expert", None),
    )
    return jax.shard_map(
        shards,
        mesh=mesh,
        in_specs=placed,
        out_specs=(P("dp", "expert", None), P("dp", "expert", None), P("dp", "expert", None)),
        check_vma=False,
    )
```

```python
import functools

import jax
import jax.numpy as jnp
from jax import lax
from jax.experimental import pallas as pl
from jax.experimental.pallas import tpu as pltpu
from jax.sharding import PartitionSpec as P

beta_one = 0.9
beta_two = 0.999
learning_rate = 0.001
epsilon = 1e-08
decay_rate = 0.1
step_count = 4.0

MESH = pl.DeviceIdType.MESH
LANES = 128
CHUNK = 128
SLOTS = 4


def gradient_kernel(
    dp,
    groups,
    ids_ref,
    weights_ref,
    cot_hbm,
    hidden_hbm,
    grad_ref,
    cot,
    hidden,
    turned,
    onehot,
    slot_weight,
    send,
    recv,
    part,
    pair_recv,
    peer_recv,
    own_sum,
    load_sem,
    send_sem,
    recv_sem,
    pair_sem,
    peer_send_sem,
    peer_recv_sem,
):
    d = lax.axis_index("dp")
    s = lax.axis_index("expert")
    half = dp // 2
    parity = lax.rem(d, 2)
    q = d // 2
    partner = d + 1 - 2 * parity
    chunks, width = recv.shape[0], recv.shape[-1]
    local_count, capacity = recv.shape[2], recv.shape[3]
    top, tokens = ids_ref.shape
    rows = groups * capacity
    own = own_sum.shape[2]
    stride = chunks * (width // LANES) * local_count
    hidden_units = turned.shape[1]

    load_cot = pltpu.make_async_copy(cot_hbm, cot, load_sem.at[0])
    load_hidden = pltpu.make_async_copy(hidden_hbm, hidden, load_sem.at[1])
    load_cot.start()
    load_hidden.start()

    barrier = pltpu.get_barrier_semaphore()
    for j in range(1, groups):
        pl.semaphore_signal(
            barrier, inc=1, device_id=(d, lax.rem(s + j, groups)), device_id_type=MESH
        )
    pl.semaphore_signal(barrier, inc=1, device_id=(partner, s), device_id_type=MESH)
    for j in range(1, half):
        pl.semaphore_signal(
            barrier,
            inc=1,
            device_id=(lax.rem(q + j, half) * 2 + parity, s),
            device_id_type=MESH,
        )

    window = groups * local_count
    ids = ids_ref[...]
    weights = weights_ref[...]
    lane = lax.broadcasted_iota(jnp.int32, (window, tokens), 1)
    chosen, picked = [], []
    for k in range(window):
        hit = ids == k
        chosen.append(jnp.sum(hit.astype(jnp.int32), axis=0, keepdims=True))
        picked.append(jnp.sum(jnp.where(hit, weights, 0.0), axis=0, keepdims=True))
    count = jnp.concatenate(chosen, axis=0)
    total = count
    shift = 1
    while shift < tokens:
        total = total + jnp.where(lane >= shift, pltpu.roll(total, shift, 1), 0)
        shift *= 2
    rank = jnp.where(count > 0, total - count, -1)
    for k in range(window):
        group, local = k // local_count, k % local_count
        slot = lax.broadcasted_iota(jnp.int32, (capacity, tokens), 0)
        match = slot == rank[k : k + 1, :]
        onehot[group, pl.ds(local * capacity, capacity), :] = jnp.where(match, 1.0, 0.0).astype(
            jnp.bfloat16
        )
        value = jnp.sum(jnp.where(match, picked[k], 0.0), axis=1, keepdims=True)
        slot_weight[group, pl.ds(local * capacity, capacity), :] = jnp.broadcast_to(
            value, (capacity, LANES)
        )

    pl.semaphore_wait(barrier, groups + half - 1)
    load_cot.wait()

    def exchange(c, j):
        return pltpu.make_async_remote_copy(
            src_ref=send.at[c, j - 1],
            dst_ref=recv.at[c, s],
            send_sem=send_sem.at[c, j - 1],
            recv_sem=recv_sem.at[c, j - 1],
            device_id=(d, lax.rem(s + j, groups)),
            device_id_type=MESH,
        )

    def pair(c):
        return pltpu.make_async_remote_copy(
            src_ref=part.at[lax.rem(c, SLOTS), 1 - parity],
            dst_ref=pair_recv.at[lax.rem(c, SLOTS)],
            send_sem=pair_sem.at[c, 0],
            recv_sem=pair_sem.at[c, 1],
            device_id=(partner, s),
            device_id_type=MESH,
        )

    def peer(c, j):
        to = lax.rem(q + j, half)
        return pltpu.make_async_remote_copy(
            src_ref=part.at[lax.rem(c, SLOTS), parity, to],
            dst_ref=peer_recv.at[lax.rem(c, SLOTS), j - 1],
            send_sem=peer_send_sem.at[c, j - 1],
            recv_sem=peer_recv_sem.at[c, j - 1],
            device_id=(to * 2 + parity, s),
            device_id_type=MESH,
        )

    order = sorted(range(1, groups), key=lambda j: abs(j - groups / 2)) + [0]

    def dispatch(c, carry):
        columns = cot[:, pl.ds(pl.multiple_of(c * width, width), width)]
        for j in order:
            group = lax.rem(s + j, groups)
            taken = jnp.dot(onehot[group], columns, preferred_element_type=jnp.float32)
            block = (taken * slot_weight[group][:, :1]).astype(jnp.bfloat16)
            block = block.reshape(local_count, capacity, width)
            if j:
                send[c, j - 1] = block
                exchange(c, j).start()
            else:
                recv[c, s] = block
        return carry

    lax.fori_loop(0, chunks, dispatch, 0)

    load_hidden.wait()
    for local in range(local_count):

        def turn(i, carry, local=local):
            at = pl.ds(pl.multiple_of(i * LANES, LANES), LANES)
            turned[local, at, :] = hidden[local, :, at].T
            return carry

        lax.fori_loop(0, hidden_units // LANES, turn, 0)

    def finish(c):
        total = own_sum[lax.rem(c, SLOTS)]
        for j in range(1, half):
            peer(c, j).wait_recv()
            total = total + peer_recv[lax.rem(c, SLOTS), j - 1].astype(jnp.float32)
        for local in range(local_count):
            for tile in range(width // LANES):
                first = (c * (width // LANES) + tile) * local_count + local
                grad_ref[pl.ds(first, own, stride=stride), :] = total[
                    local, :, tile * LANES : (tile + 1) * LANES
                ]

    def combine(c):
        slot = lax.rem(c, SLOTS)
        pair(c).wait_recv()
        for j in list(range(1, half)) + [0]:
            to = lax.rem(q + j, half)
            both = part[slot, parity, to].astype(jnp.float32) + pair_recv[slot, to].astype(
                jnp.float32
            )
            if j:
                part[slot, parity, to] = both.astype(jnp.bfloat16)
                peer(c, j).start()
            else:
                own_sum[slot] = both

    def sent(c):
        pair(c).wait_send()
        for j in range(1, half):
            peer(c, j).wait_send()

    def behind(c):
        @pl.when(c > 0)
        def _():
            combine(c - 1)

        @pl.when(c > 1)
        def _():
            finish(c - 2)

    def step(ahead, c, carry):
        if ahead:
            behind(c)
        slot = lax.rem(c, SLOTS)

        @pl.when(c >= SLOTS)
        def _():
            sent(c - SLOTS)

        for j in range(1, groups):
            exchange(c, j).wait_recv()
        for local in range(local_count):
            held = recv[c, :, local].reshape(rows, width)
            product = jnp.dot(turned[local], held, preferred_element_type=jnp.float32)
            for block in range(dp):
                part[slot, block % 2, block // 2, local] = product[
                    block * own : (block + 1) * own
                ].astype(jnp.bfloat16)
        pair(c).start()

        if not ahead:
            behind(c)
        return carry

    turn_at = chunks * 3 // 4
    lax.fori_loop(0, turn_at, functools.partial(step, False), 0)
    lax.fori_loop(turn_at, chunks, functools.partial(step, True), 0)
    combine(chunks - 1)
    if chunks > 1:
        finish(chunks - 2)
    finish(chunks - 1)

    def drain(c, carry):
        for j in range(1, groups):
            exchange(c, j).wait_send()
        return carry

    for c in range(max(chunks - SLOTS, 0), chunks):
        sent(c)
    lax.fori_loop(0, chunks, drain, 0)


def gradient_sum(dp, groups, cotangent, route_ids, route_weights, hidden, own):
    tokens, depth = cotangent.shape
    local_count, rows, hidden_units = hidden.shape
    capacity = rows // groups
    window = local_count * groups
    chunks = depth // CHUNK
    half = dp // 2
    top = route_ids.shape[1]
    vmem = pl.BlockSpec(memory_space=pltpu.VMEM)
    anywhere = pl.BlockSpec(memory_space=pltpu.HBM)
    dma = pltpu.SemaphoreType.DMA
    return pl.pallas_call(
        functools.partial(gradient_kernel, dp, groups),
        out_shape=jax.ShapeDtypeStruct((own * depth * local_count // LANES, LANES), jnp.float32),
        in_specs=[vmem, vmem, anywhere, anywhere],
        out_specs=vmem,
        scratch_shapes=[
            pltpu.VMEM((tokens, depth), jnp.bfloat16),
            pltpu.VMEM(hidden.shape, jnp.bfloat16),
            pltpu.VMEM((local_count, hidden_units, rows), jnp.bfloat16),
            pltpu.VMEM((groups, local_count * capacity, tokens), jnp.bfloat16),
            pltpu.VMEM((groups, local_count * capacity, LANES), jnp.float32),
            pltpu.VMEM((chunks, groups - 1, local_count, capacity, CHUNK), jnp.bfloat16),
            pltpu.VMEM((chunks, groups, local_count, capacity, CHUNK), jnp.bfloat16),
            pltpu.VMEM((SLOTS, 2, half, local_count, own, CHUNK), jnp.bfloat16),
            pltpu.VMEM((SLOTS, half, local_count, own, CHUNK), jnp.bfloat16),
            pltpu.VMEM((SLOTS, half - 1, local_count, own, CHUNK), jnp.bfloat16),
            pltpu.VMEM((SLOTS, local_count, own, CHUNK), jnp.float32),
            dma((2,)),
            dma((chunks, groups - 1)),
            dma((chunks, groups - 1)),
            dma((chunks, 2)),
            dma((chunks, half - 1)),
            dma((chunks, half - 1)),
        ],
        compiler_params=pltpu.CompilerParams(
            collective_id=0, has_side_effects=True, vmem_limit_bytes=50 * 1024 * 1024
        ),
    )(route_ids.T, route_weights.T, cotangent, hidden)


def solution(mesh):
    dp, groups = mesh.shape["dp"], mesh.shape["expert"]

    def shards(cotangent, route_ids, route_weights, hidden, master, first_moment, second_moment):
        capacity = hidden.shape[1] // groups
        summed = gradient_sum(
            dp, groups, cotangent, route_ids, route_weights, hidden, master.shape[0]
        )
        shape = master.shape
        split = (shape[0], shape[1], shape[2] // LANES, LANES)

        def flat(x):
            return x.reshape(split).transpose(0, 2, 1, 3).reshape(-1, LANES)

        def whole(x):
            return x.reshape(split[0], split[2], split[1], LANES).transpose(0, 2, 1, 3).reshape(shape)

        master, first_moment, second_moment = lax.optimization_barrier(
            (flat(master), flat(first_moment), flat(second_moment))
        )
        gradient = summed / jnp.sqrt(jnp.float32(groups * capacity))
        new_first = beta_one * first_moment + (1.0 - beta_one) * gradient
        new_second = beta_two * second_moment + (1.0 - beta_two) * gradient * gradient
        corrected_first = new_first / (1.0 - beta_one**step_count)
        corrected_second = new_second / (1.0 - beta_two**step_count)
        update = corrected_first / (jnp.sqrt(corrected_second) + epsilon) + decay_rate * master
        new_master = master - learning_rate * update
        return (whole(new_master), whole(new_first), whole(new_second))

    placed = (
        P(("dp", "expert"), None),
        P(("dp", "expert"), None),
        P(("dp", "expert"), None),
        P("expert", "dp", None),
        P("dp", "expert", None),
        P("dp", "expert", None),
        P("dp", "expert", None),
    )
    return jax.shard_map(
        shards,
        mesh=mesh,
        in_specs=placed,
        out_specs=(P("dp", "expert", None), P("dp", "expert", None), P("dp", "expert", None)),
        check_vma=False,
    )
```
